32 devices in a mesh: tp: 8 (over y, x, core), dp: 4 (over z).
Axes of the slice: x: 2, y: 2, z: 4, core: 2. Of those that a mesh axis runs over, the one named last changes fastest.
Arguments:
- grad_out: bfloat16 [1792, 8192], P(('dp', 'tp')), may hold values from -6 to 6
- gate_act: bfloat16 [1792, 14336], P('dp', 'tp'), may hold values from -8 to 8
- up_act: bfloat16 [1792, 14336], P('dp', 'tp'), may hold values from -6 to 6
- down_weight: bfloat16 [14336, 8192], P('tp'), may hold values from -0.0625 to 0.0625
Outputs:
- grad_gate: bfloat16 [1792, 14336], P('dp', 'tp')
- grad_up: bfloat16 [1792, 14336], P('dp', 'tp')
- grad_down: bfloat16 [14336, 8192], P(('tp', 'dp'))
The draws below stay inside these ranges and needn't reach their ends.
All inputs are finite; a program needn't handle non-finite values.
Results may differ from the reference program's by a relative error of at most 0.013.
Values may be sent and summed in bfloat16 or wider, within the bound.
No kernel may reach another device: no remote copies, remote signals or barrier semaphores. Data moves between devices by JAX's collectives and lax.ppermute only.
A program may use at most 128 MiB of HBM per device.

```python
import math
import jax
import jax.numpy as jnp
from jax import lax

D = 8192
FF = 14336
GROUP = 448
TOKENS = 1792
N_DP = 4


def block_scale(stream_key, extent, shards, low, high):
    def one(axis_at, shards_of):
        draws = jax.random.uniform(jax.random.fold_in(jax.random.fold_in(stream_key, 6), axis_at), (shards_of,), jnp.float32, low / len(shards), high / len(shards))
        return jnp.repeat(jnp.exp(draws), extent[axis_at] // shards_of).reshape((-1,) + (1,) * (len(extent) - axis_at - 1))

    gain = one(*shards[0])
    for cut in shards[1:]:
        gain = gain * one(*cut)
    return gain


def gaussian(own_key, dims, width, limit, shards=(), dtype=jnp.bfloat16):
    array = jax.random.normal(own_key, dims, jnp.float32) * width
    if len(shards) > 0:
        array = block_scale(own_key, dims, shards, -0.22, 0.18) * array
    return jnp.clip(array, min=-limit, max=limit).astype(dtype)


def setup_inputs(seed: int = 0) -> dict:
    keys = jax.random.split(jax.random.key(seed), 5)
    return {
        "grad_out": gaussian(keys[0], (TOKENS, D), 1.0, 6.0, ((0, 32),)),
        "gate_act": gaussian(keys[1], (TOKENS, FF), 1.5, 8.0, ((0, 4), (1, 8))),
        "up_act": gaussian(keys[2], (TOKENS, FF), 1.0, 6.0, ((0, 4), (1, 8))),
        "down_weight": gaussian(keys[3], (FF, D), D ** -0.5, 0.0625, ((0, 8),)),
    }


def reference(grad_out, gate_act, up_act, down_weight):
    gate_val = gate_act.astype(jnp.float32)
    up_val = up_act.astype(jnp.float32)
    squash = jax.nn.sigmoid(gate_val)
    hidden = (gate_val * squash * up_val).astype(jnp.bfloat16)
    grad_hidden = jnp.dot(grad_out, down_weight.T, preferred_element_type=jnp.float32)
    grad_gate = (grad_hidden * up_val * squash * (1.0 + gate_val * (1.0 - squash))).astype(jnp.bfloat16)
    grad_up = (grad_hidden * gate_val * squash).astype(jnp.bfloat16)
    hid_groups = hidden.reshape(N_DP, GROUP, FF)
    out_groups = grad_out.reshape(N_DP, GROUP, D)

    def add_group(running, pair):
        partial_value = jnp.dot(pair[0].T, pair[1], preferred_element_type=jnp.float32).astype(jnp.bfloat16)
        partial_value = lax.optimization_barrier(partial_value)
        return (running + partial_value.astype(jnp.float32), None)
    running, unused = lax.scan(add_group, jnp.zeros((FF, D), jnp.float32), (hid_groups, out_groups))
    grad_scale = 1.0 / math.sqrt(TOKENS)
    grad_down = (running * grad_scale).astype(jnp.bfloat16)
    return (grad_gate, grad_up, grad_down)
```

```python
import functools
import math

import jax
import jax.numpy as jnp
from jax import lax
from jax.experimental import pallas as pl
from jax.experimental.pallas import tpu as pltpu
from jax.sharding import PartitionSpec as P

AXES = ("tp", "dp")


def scatter_body(grad_out, gate_act, up_act, down_weight):
    gate_val = gate_act.astype(jnp.float32)
    up_val = up_act.astype(jnp.float32)
    squash = jax.nn.sigmoid(gate_val)
    hidden = (gate_val * squash * up_val).astype(jnp.bfloat16)
    incoming = lax.all_gather(grad_out, "tp", axis=0, tiled=True)
    grad_hidden = lax.dot_general(
        incoming, down_weight, (((1,), (1,)), ((), ())), preferred_element_type=jnp.float32
    )
    weight_part = lax.dot_general(
        hidden, incoming, (((0,), (0,)), ((), ())), preferred_element_type=jnp.float32
    )
    summed = lax.psum_scatter(
        weight_part.astype(jnp.bfloat16), "dp", scatter_dimension=0, tiled=True
    ).astype(jnp.float32)
    grad_gate = (grad_hidden * up_val * squash * (1.0 + gate_val * (1.0 - squash))).astype(
        jnp.bfloat16
    )
    grad_up = (grad_hidden * gate_val * squash).astype(jnp.bfloat16)
    token_total = grad_out.shape[0] * lax.axis_size("tp") * lax.axis_size("dp")
    grad_down = (summed * (1.0 / math.sqrt(token_total))).astype(jnp.bfloat16)
    return (grad_gate, grad_up, grad_down)


def chip_slot(place, own_half, piece):
    chip, core = place[0], place[1]
    side = core if own_half else 1 - core
    if piece == 0:
        return chip
    if piece == 3:
        return chip ^ 3
    return chip ^ (piece + side * (3 - 2 * piece))


def hidden_kernel(place, gate_ref, up_ref, weight_ref, *refs, rows, half):
    pieces, (grad_gate_ref, grad_up_ref, store, sems) = refs[:8], refs[8:]
    core = place[1]

    def copies():
        out = []
        for i, piece in enumerate(pieces):
            side, which = i // 4, i % 4
            column_half = core ^ side
            out.append(
                pltpu.make_async_copy(
                    piece,
                    store.at[column_half, chip_slot(place, side == 0, which)],
                    sems.at[i],
                )
            )
        return out

    @pl.when(pl.program_id(0) == 0)
    def _():
        for copy in copies():
            copy.start()
        for copy in copies():
            copy.wait()

    depth = half // 4
    total = None
    for h in range(2):
        for k in range(4):
            left = store[h, :, :, k * depth : (k + 1) * depth].reshape(4 * rows, depth)
            right = weight_ref[:, h * half + k * depth : h * half + (k + 1) * depth]
            term = lax.dot_general(
                left, right, (((1,), (1,)), ((), ())), preferred_element_type=jnp.float32
            )
            total = term if total is None else total + term
    gate_val = gate_ref[...].astype(jnp.float32)
    up_val = up_ref[...].astype(jnp.float32)
    squash = jax.nn.sigmoid(gate_val)
    grad_gate_ref[...] = (
        total * up_val * squash * (1.0 + gate_val * (1.0 - squash))
    ).astype(jnp.bfloat16)
    grad_up_ref[...] = (total * gate_val * squash).astype(jnp.bfloat16)


def hidden_grads(place, gate_act, up_act, down_weight, pieces):
    rows, half = pieces[0].shape
    tokens, units = gate_act.shape
    width = down_weight.shape[1]
    tile = 256
    spec = pl.BlockSpec((tokens, tile), lambda i, place: (0, i))
    return pl.pallas_call(
        functools.partial(hidden_kernel, rows=rows, half=half),
        out_shape=[jax.ShapeDtypeStruct((tokens, units), jnp.bfloat16)] * 2,
        grid_spec=pltpu.PrefetchScalarGridSpec(
            num_scalar_prefetch=1,
            grid=(units // tile,),
            in_specs=[spec, spec, pl.BlockSpec((tile, width), lambda i, place: (i, 0))]
            + [pl.BlockSpec(memory_space=pl.ANY)] * 8,
            out_specs=[spec, spec],
            scratch_shapes=[
                pltpu.VMEM((2, 4, rows, half), jnp.bfloat16),
                pltpu.SemaphoreType.DMA((8,)),
            ],
        ),
        cost_estimate=pl.CostEstimate(
            flops=2 * tokens * units * width,
            bytes_accessed=2 * (units * width + tokens * width + 4 * tokens * units),
            transcendentals=tokens * units,
        ),
        name="hidden_grads",
    )(place, gate_act, up_act, down_weight, *pieces)


def down_kernel(place, left_ref, *refs, rows, planes, tile, start, steps, scale, aliased):
    near, far = refs[:8], refs[8:16]
    out_ref, store, sems = refs[16 + aliased :]
    step = pl.program_id(0)

    def copies(side, index, slot):
        out = []
        for which in range(4):
            chip = chip_slot(place, side == 0, which)
            i = side * 4 + which
            at = pl.multiple_of(index * tile, 128)
            out.append(
                pltpu.make_async_copy(
                    near[i].at[:, pl.ds(start + at, tile)],
                    store.at[slot, 0, chip],
                    sems.at[slot, which],
                )
            )
            out.append(
                pltpu.make_async_copy(
                    far[i].at[:, :, pl.ds(at, tile)],
                    store.at[slot, pl.ds(1, planes - 1), chip],
                    sems.at[slot, 4 + which],
                )
            )
        return out

    def fetch(at):
        for side in range(2):

            @pl.when(at // steps == side)
            def _():
                for copy in copies(side, at - side * steps, at % 2):
                    copy.start()

    @pl.when(step == 0)
    def _():
        fetch(step)

    @pl.when(step + 1 < 2 * steps)
    def _():
        fetch(step + 1)

    for copy in copies(0, 0, step % 2):
        copy.wait()
    right = store[step % 2].reshape(planes * 4 * rows, tile)
    out_ref[...] = (
        jnp.dot(left_ref[...], right, preferred_element_type=jnp.float32) * scale
    ).astype(jnp.bfloat16)


def down_grads(place, left, near, far, start, scale, result):
    rows, half = near[0].shape
    planes = far[0].shape[0] + 1
    chunk = far[0].shape[2]
    units, depth = left.shape
    tile = 512
    steps = chunk // tile
    aliased = result is not None

    def out_at(i, place):
        column_half = place[1] ^ (i // steps)
        return (0, (column_half * half + start) // tile + i % steps)

    return pl.pallas_call(
        functools.partial(
            down_kernel,
            rows=rows,
            planes=planes,
            tile=tile,
            start=start,
            steps=steps,
            scale=scale,
            aliased=int(aliased),
        ),
        out_shape=jax.ShapeDtypeStruct((units, 2 * half), jnp.bfloat16),
        grid_spec=pltpu.PrefetchScalarGridSpec(
            num_scalar_prefetch=1,
            grid=(2 * steps,),
            in_specs=[pl.BlockSpec((units, depth), lambda i, place: (0, 0))]
            + [pl.BlockSpec(memory_space=pl.ANY)] * (16 + int(aliased)),
            out_specs=pl.BlockSpec((units, tile), out_at),
            scratch_shapes=[
                pltpu.VMEM((2, planes, 4, rows, tile), jnp.bfloat16),
                pltpu.SemaphoreType.DMA((2, 8)),
            ],
        ),
        input_output_aliases={18: 0} if aliased else {},
        cost_estimate=pl.CostEstimate(
            flops=2 * units * depth * 2 * chunk,
            bytes_accessed=2 * (units * depth + (units + depth) * 2 * chunk),
            transcendentals=0,
        ),
        name="down_grads",
    )(place, left, *near, *far, *([result] if aliased else []))


def gather_body(n_tp, n_dp, grad_out, gate_act, up_act, down_weight):
    own_rows, width = grad_out.shape
    half = width // 2
    units = gate_act.shape[1]
    share = units // n_dp
    scale = 1.0 / math.sqrt(own_rows * n_tp * n_dp)
    tp = lax.axis_index("tp")
    dp = lax.axis_index("dp")
    core = tp % 2
    place = jnp.stack([tp // 2, core]).astype(jnp.int32)

    def send(value, target):
        pairs = []
        for t in range(n_tp):
            for d in range(n_dp):
                to_t, to_d = target(t, d)
                pairs.append((t * n_dp + d, to_t * n_dp + to_d))
        return lax.ppermute(value, AXES, pairs)

    def swap_core(value):
        return send(value, lambda t, d: (t ^ 1, d))

    def first_link(value):
        return send(value, lambda t, d: (t ^ (4 if t % 2 else 2), d))

    def second_link(value):
        return send(value, lambda t, d: (t ^ (2 if t % 2 else 4), d))

    def shift(value, by):
        return send(value, lambda t, d: (t, (d + by) % n_dp))

    mine = lax.dynamic_slice_in_dim(grad_out, core * half, half, 1)
    other = swap_core(lax.dynamic_slice_in_dim(grad_out, (1 - core) * half, half, 1))
    block = jnp.where(
        core == 0,
        jnp.concatenate([mine, other], 0),
        jnp.concatenate([other, mine], 0),
    )
    rows = 2 * own_rows

    unit = half // 8
    sizes = [3 * unit, 3 * unit, 2 * unit]
    starts = [sum(sizes[:i]) for i in range(len(sizes))]

    gate_val = gate_act.astype(jnp.float32)
    hidden = (gate_val * jax.nn.sigmoid(gate_val) * up_act.astype(jnp.float32)).astype(
        jnp.bfloat16
    )
    hidden_t = hidden.T

    near = [block, first_link(block), second_link(block)]
    near.append(second_link(near[1]))
    near += [swap_core(piece) for piece in near]

    remote = []
    for start, size in zip(starts, sizes):
        part = block[:, start : start + size]
        remote.append(jnp.stack([shift(part, s) for s in range(1, n_dp)]))

    lefts = []
    for s in range(n_dp):
        sent = lax.dynamic_slice_in_dim(hidden_t, ((dp + s) % n_dp) * share, share, 0)
        lefts.append(shift(sent, s) if s else sent)
    left = jnp.concatenate(lefts, 1)

    grad_gate, grad_up = hidden_grads(place, gate_act, up_act, down_weight, near)

    grad_down = None
    for start, size, piece in zip(starts, sizes, remote):
        far = [piece, first_link(piece), second_link(piece)]
        far.append(second_link(far[1]))
        far += [swap_core(value) for value in far]
        grad_down = down_grads(place, left, near, far, start, scale, grad_down)
    return (grad_gate, grad_up, grad_down)


def solution(mesh):
    n_tp, n_dp = mesh.shape["tp"], mesh.shape["dp"]

    def body(grad_out, gate_act, up_act, down_weight):
        tokens = grad_out.shape[0] * n_tp * n_dp
        if n_tp == 8 and tokens <= down_weight.shape[0]:
            return gather_body(n_tp, n_dp, grad_out, gate_act, up_act, down_weight)
        return scatter_body(grad_out, gate_act, up_act, down_weight)

    return jax.shard_map(
        body,
        mesh=mesh,
        in_specs=(P(("dp", "tp"), None), P("dp", "tp"), P("dp", "tp"), P("tp", None)),
        out_specs=(P("dp", "tp"), P("dp", "tp"), P(("tp", "dp"), None)),
        check_vma=False,
    )
```

```python
import functools
import math

import jax
import jax.numpy as jnp
from jax import lax
from jax.experimental import pallas as pl
from jax.experimental.pallas import tpu as pltpu
from jax.sharding import PartitionSpec as P


AXES = ("tp", "dp")


def scatter_body(grad_out, gate_act, up_act, down_weight):
    gate_val = gate_act.astype(jnp.float32)
    up_val = up_act.astype(jnp.float32)
    squash = jax.nn.sigmoid(gate_val)
    hidden = (gate_val * squash * up_val).astype(jnp.bfloat16)
    incoming = lax.all_gather(grad_out, "tp", axis=0, tiled=True)
    grad_hidden = lax.dot_general(
        incoming, down_weight, (((1,), (1,)), ((), ())), preferred_element_type=jnp.float32
    )
    weight_part = lax.dot_general(
        hidden, incoming, (((0,), (0,)), ((), ())), preferred_element_type=jnp.float32
    )
    summed = lax.psum_scatter(
        weight_part.astype(jnp.bfloat16), "dp", scatter_dimension=0, tiled=True
    ).astype(jnp.float32)
    grad_gate = (grad_hidden * up_val * squash * (1.0 + gate_val * (1.0 - squash))).astype(
        jnp.bfloat16
    )
    grad_up = (grad_hidden * gate_val * squash).astype(jnp.bfloat16)
    token_total = grad_out.shape[0] * lax.axis_size("tp") * lax.axis_size("dp")
    grad_down = (summed * (1.0 / math.sqrt(token_total))).astype(jnp.bfloat16)
    return (grad_gate, grad_up, grad_down)


def chip_slot(place, own_half, piece):
    chip, core = place[0], place[1]
    side = core if own_half else 1 - core
    if piece == 0:
        return chip
    if piece == 3:
        return chip ^ 3
    return chip ^ (piece + side * (3 - 2 * piece))


def hidden_kernel(place, gate_ref, up_ref, weight_ref, *refs, rows, half, aliased):
    pieces, (grad_gate_ref, grad_up_ref, store, sems) = refs[:8], refs[8 + aliased :]
    core = place[1]

    def copies():
        return [
            pltpu.make_async_copy(
                piece,
                store.at[core ^ (i // 4), chip_slot(place, i < 4, i % 4)],
                sems.at[i],
            )
            for i, piece in enumerate(pieces)
        ]

    @pl.when(pl.program_id(0) == 0)
    def _():
        for copy in copies():
            copy.start()
        for copy in copies():
            copy.wait()

    total = None
    for h in range(2):
        term = lax.dot_general(
            store[h].reshape(4 * rows, half),
            weight_ref[:, h * half : (h + 1) * half],
            (((1,), (1,)), ((), ())),
            preferred_element_type=jnp.float32,
        )
        total = term if total is None else total + term
    gate_val = gate_ref[...].astype(jnp.float32)
    up_val = up_ref[...].astype(jnp.float32)
    squash = jax.nn.sigmoid(gate_val)
    grad_gate_ref[...] = (
        total * up_val * squash * (1.0 + gate_val * (1.0 - squash))
    ).astype(jnp.bfloat16)
    grad_up_ref[...] = (total * gate_val * squash).astype(jnp.bfloat16)


def hidden_grads(place, gate_act, up_act, down_weight, pieces, lo, count, results):
    rows, half = pieces[0].shape
    tokens, units = gate_act.shape
    width = down_weight.shape[1]
    tile = 256
    spec = pl.BlockSpec((tokens, tile), lambda i, place: (0, lo + i))
    aliased = len(results)
    return pl.pallas_call(
        functools.partial(hidden_kernel, rows=rows, half=half, aliased=aliased),
        out_shape=[jax.ShapeDtypeStruct((tokens, units), jnp.bfloat16)] * 2,
        grid_spec=pltpu.PrefetchScalarGridSpec(
            num_scalar_prefetch=1,
            grid=(count,),
            in_specs=[spec, spec, pl.BlockSpec((tile, width), lambda i, place: (lo + i, 0))]
            + [pl.BlockSpec(memory_space=pl.ANY)] * (8 + aliased),
            out_specs=[spec, spec],
            scratch_shapes=[
                pltpu.VMEM((2, 4, rows, half), jnp.bfloat16),
                pltpu.SemaphoreType.DMA((8,)),
            ],
        ),
        input_output_aliases={12: 0, 13: 1} if aliased else {},
        cost_estimate=pl.CostEstimate(
            flops=2 * tokens * count * tile * width,
            bytes_accessed=2 * (count * tile * width + tokens * width),
            transcendentals=tokens * count * tile,
        ),
        compiler_params=pltpu.CompilerParams(vmem_limit_bytes=28 << 20),
        name="hidden_grads",
    )(place, gate_act, up_act, down_weight, *pieces, *results)


def down_kernel(place, *refs, rows, planes, tile, start, steps, scale, wide, aliased):
    count = 4 + (planes - 1 if wide else 4)
    near, far, lefts = refs[:4], refs[4:count], refs[count : count + 2]
    out_ref, other_ref, store, left, sems, left_sems = refs[count + 2 + aliased :]
    step = pl.program_id(0)
    units = out_ref.shape[0]

    def copies(index, slot):
        out = []
        for which in range(4):
            chip = chip_slot(place, True, which)
            at = pl.multiple_of(index * tile, 128)
            out.append(
                pltpu.make_async_copy(
                    near[which].at[:, pl.ds(start + at, tile)],
                    store.at[slot, 0, chip],
                    sems.at[slot, which],
                )
            )
            if wide:
                for s in range(1, planes):
                    out.append(
                        pltpu.make_async_copy(
                            far[s - 1].at[which, :, pl.ds(at, tile)],
                            store.at[slot, s, chip],
                            sems.at[slot, s * 4 + which],
                        )
                    )
            else:
                out.append(
                    pltpu.make_async_copy(
                        far[which].at[:, :, pl.ds(at, tile)],
                        store.at[slot, pl.ds(1, planes - 1), chip],
                        sems.at[slot, 4 + which],
                    )
                )
        return out

    def left_copies():
        return [
            pltpu.make_async_copy(ref, left.at[pl.ds(i * units, units)], left_sems.at[i])
            for i, ref in enumerate(lefts)
        ]

    @pl.when(step == 0)
    def _():
        for copy in copies(0, 0) + left_copies():
            copy.start()

    @pl.when(step + 1 < steps)
    def _():
        for copy in copies(step + 1, (step + 1) % 2):
            copy.start()

    @pl.when(step == 0)
    def _():
        for copy in left_copies():
            copy.wait()

    for copy in copies(0, step % 2):
        copy.wait()
    right = store[step % 2].reshape(planes * 4 * rows, tile)
    both = jnp.dot(left[...], right, preferred_element_type=jnp.float32) * scale
    out_ref[...] = both[:units].astype(jnp.bfloat16)
    other_ref[...] = both[units:].astype(jnp.bfloat16)


def down_grads(place, lefts, near, far, start, scale, wide, result):
    rows, half = near[0].shape
    planes = lefts[0].shape[1] // (4 * rows)
    chunk = far[0].shape[2]
    units, depth = lefts[0].shape
    tile = 512
    steps = chunk // tile
    aliased = int(result is not None)
    return pl.pallas_call(
        functools.partial(
            down_kernel,
            rows=rows,
            planes=planes,
            tile=tile,
            start=start,
            steps=steps,
            scale=scale,
            wide=wide,
            aliased=aliased,
        ),
        out_shape=[
            jax.ShapeDtypeStruct((units, 2 * half), jnp.bfloat16),
            jax.ShapeDtypeStruct((units, chunk), jnp.bfloat16),
        ],
        grid_spec=pltpu.PrefetchScalarGridSpec(
            num_scalar_prefetch=1,
            grid=(steps,),
            in_specs=[pl.BlockSpec(memory_space=pl.ANY)] * (6 + len(far) + aliased),
            out_specs=[
                pl.BlockSpec(
                    (units, tile), lambda i, place: (0, (place[1] * half + start) // tile + i)
                ),
                pl.BlockSpec((units, tile), lambda i, place: (0, i)),
            ],
            scratch_shapes=[
                pltpu.VMEM((2, planes, 4, rows, tile), jnp.bfloat16),
                pltpu.VMEM((2 * units, depth), jnp.bfloat16),
                pltpu.SemaphoreType.DMA((2, 4 * planes)),
                pltpu.SemaphoreType.DMA((2,)),
            ],
        ),
        input_output_aliases={7 + len(far): 0} if aliased else {},
        cost_estimate=pl.CostEstimate(
            flops=4 * units * depth * chunk,
            bytes_accessed=2 * (2 * units * depth + (2 * units + depth) * chunk),
            transcendentals=0,
        ),
        compiler_params=pltpu.CompilerParams(vmem_limit_bytes=20 << 20),
        name="down_grads",
    )(place, *near, *far, *lefts, *([result] if aliased else []))


def place_kernel(place, value_ref, result_ref, out_ref, store, in_sems, out_sems, *, start, tile):
    _, chunk = value_ref.shape
    half = out_ref.shape[1] // 2
    base = (1 - place[1]) * half + start
    ins, outs = [], []
    for i in range(chunk // tile):
        part = store.at[i]
        at = pl.multiple_of(base + i * tile, 128)
        ins.append(
            pltpu.make_async_copy(
                value_ref.at[:, pl.ds(i * tile, tile)], part, in_sems.at[i]
            )
        )
        outs.append(
            pltpu.make_async_copy(part, out_ref.at[:, pl.ds(at, tile)], out_sems.at[i])
        )
    for copy in ins:
        copy.start()
    for into, out in zip(ins, outs):
        into.wait()
        out.start()
    for out in outs:
        out.wait()


def place_other(place, value, result, start):
    units, chunk = value.shape
    tile = 512
    parts = chunk // tile
    return pl.pallas_call(
        functools.partial(place_kernel, start=start, tile=tile),
        out_shape=jax.ShapeDtypeStruct(result.shape, result.dtype),
        grid_spec=pltpu.PrefetchScalarGridSpec(
            num_scalar_prefetch=1,
            grid=(),
            in_specs=[pl.BlockSpec(memory_space=pl.ANY)] * 2,
            out_specs=pl.BlockSpec(memory_space=pl.ANY),
            scratch_shapes=[
                pltpu.VMEM((parts, units, tile), jnp.bfloat16),
                pltpu.SemaphoreType.DMA((parts,)),
                pltpu.SemaphoreType.DMA((parts,)),
            ],
        ),
        input_output_aliases={2: 0},
        cost_estimate=pl.CostEstimate(
            flops=0, bytes_accessed=4 * units * chunk, transcendentals=0
        ),
        compiler_params=pltpu.CompilerParams(vmem_limit_bytes=8 << 20),
        name="place_other",
    )(place, value, result)


def left_kernel(*refs, planes):
    pieces, (out_ref, store, sems) = refs[:planes], refs[planes:]
    tokens = store.shape[0] // planes
    copies = [
        pltpu.make_async_copy(piece, store.at[pl.ds(s * tokens, tokens)], sems.at[s])
        for s, piece in enumerate(pieces)
    ]
    for copy in copies:
        copy.start()
    for copy in copies:
        copy.wait()
    for k in range(0, planes * tokens, 256):
        out_ref[:, k : k + 256] = store[k : k + 256, :].T


def assemble_left(pieces):
    planes = len(pieces)
    tokens, share = pieces[0].shape
    return pl.pallas_call(
        functools.partial(left_kernel, planes=planes),
        out_shape=jax.ShapeDtypeStruct((share, planes * tokens), jnp.bfloat16),
        in_specs=[pl.BlockSpec(memory_space=pl.ANY)] * planes,
        out_specs=pl.BlockSpec(memory_space=pltpu.VMEM),
        scratch_shapes=[
            pltpu.VMEM((planes * tokens, share), jnp.bfloat16),
            pltpu.SemaphoreType.DMA((planes,)),
        ],
        cost_estimate=pl.CostEstimate(
            flops=0, bytes_accessed=4 * planes * tokens * share, transcendentals=0
        ),
        compiler_params=pltpu.CompilerParams(vmem_limit_bytes=8 << 20),
        name="assemble_left",
    )(*pieces)


UNITS = (4, 3, 1)
HIDDEN_CALLS = 1
RELAYED = (True, True, False)
WIDE = (False, False, True)


def gather_body(n_tp, n_dp, grad_out, gate_act, up_act, down_weight):
    own_rows, width = grad_out.shape
    half = width // 2
    units = gate_act.shape[1]
    share = units // n_dp
    scale = 1.0 / math.sqrt(own_rows * n_tp * n_dp)
    tp = lax.axis_index("tp")
    dp = lax.axis_index("dp")
    core = tp & 1
    place = jnp.stack([tp >> 1, core]).astype(jnp.int32)

    def send(value, target):
        pairs = []
        for t in range(n_tp):
            for d in range(n_dp):
                to_t, to_d = target(t, d)
                pairs.append((t * n_dp + d, to_t * n_dp + to_d))
        return lax.ppermute(value, AXES, pairs)

    def swap_core(value):
        return send(value, lambda t, d: (t ^ 1, d))

    def first_link(value):
        return send(value, lambda t, d: (t ^ (4 if t % 2 else 2), d))

    def second_link(value):
        return send(value, lambda t, d: (t ^ (2 if t % 2 else 4), d))

    def shift(value, by):
        return send(value, lambda t, d: (t, (d + by) % n_dp))

    mine = lax.dynamic_slice_in_dim(grad_out, core * half, half, 1)
    other = swap_core(lax.dynamic_slice_in_dim(grad_out, (1 - core) * half, half, 1))
    block = jnp.where(
        core == 0,
        jnp.concatenate([mine, other], 0),
        jnp.concatenate([other, mine], 0),
    )

    sizes = [n * (half // sum(UNITS)) for n in UNITS]
    starts = [sum(sizes[:i]) for i in range(len(sizes))]

    near = [block, first_link(block), second_link(block)]
    near.append(second_link(near[1]))
    near += [swap_core(piece) for piece in near]

    remote = []
    for k, (start, size) in enumerate(zip(starts, sizes)):
        if WIDE[k]:
            part = jnp.stack([piece[:, start : start + size] for piece in near[:4]])
        else:
            part = block[:, start : start + size]
        one = shift(part, 1)
        last = shift(part, n_dp - 1)
        got = [one]
        for s in range(2, n_dp - 1):
            value, by = (got[-1], 1) if RELAYED[k] else (part, s)
            got.append(shift(value, by))
        got.append(last)
        remote.append(got if WIDE[k] else jnp.stack(got))

    hiddens = []
    for s in range(n_dp):
        at = ((dp + s) & (n_dp - 1)) * share
        gate_val = lax.dynamic_slice_in_dim(gate_act, at, share, 1).astype(jnp.float32)
        up_val = lax.dynamic_slice_in_dim(up_act, at, share, 1).astype(jnp.float32)
        hidden = (gate_val * jax.nn.sigmoid(gate_val) * up_val).astype(jnp.bfloat16)
        hiddens.append(hidden)
    lefts = [shift(hidden, s) if s else hidden for s, hidden in enumerate(hiddens)]
    left = assemble_left(lefts)
    lefts = [left, swap_core(left)]

    results = []
    lo = 0
    blocks = units // 256
    for i in range(HIDDEN_CALLS):
        count = (blocks - lo) // (HIDDEN_CALLS - i)
        results = hidden_grads(
            place, gate_act, up_act, down_weight, near, lo, count, results
        )
        lo += count
    grad_gate, grad_up = results

    grad_down = None
    for k, (start, piece) in enumerate(zip(starts, remote)):
        if WIDE[k]:
            far = piece
        else:
            far = [piece, first_link(piece), second_link(piece)]
            far.append(second_link(far[1]))
        grad_down, other = down_grads(place, lefts, near[:4], far, start, scale, WIDE[k], grad_down)
        other = swap_core(other)
        grad_down = place_other(place, other, grad_down, start)
    return (grad_gate, grad_up, grad_down)


def solution(mesh):
    n_tp, n_dp = mesh.shape["tp"], mesh.shape["dp"]

    def body(grad_out, gate_act, up_act, down_weight):
        tokens = grad_out.shape[0] * n_tp * n_dp
        if n_tp == 8 and n_dp == 4 and tokens <= down_weight.shape[0]:
            return gather_body(n_tp, n_dp, grad_out, gate_act, up_act, down_weight)
        return scatter_body(grad_out, gate_act, up_act, down_weight)

    return jax.shard_map(
        body,
        mesh=mesh,
        in_specs=(P(("dp", "tp"), None), P("dp", "tp"), P("dp", "tp"), P("tp", None)),
        out_specs=(P("dp", "tp"), P("dp", "tp"), P(("tp", "dp"), None)),
        check_vma=False,
    )
```
